32 devices in a mesh: gx: 4 (over z), gy: 2 (over x), gz: 4 (over y, core).
Axes of the slice: x: 2, y: 2, z: 4, core: 2. Of those that a mesh axis runs over, the one named last changes fastest.
Arguments:
- tri_geom: float32 [10, 32768], P(None, ('gx', 'gy', 'gz')), as said below
- send_index: int32 [256, 128], P(('gx', 'gy', 'gz')), may hold values from -1 to 1023, as said below
- near_index: int32 [32, 64, 512], P('gx', 'gy', 'gz'), may hold values from 0 to 1023, as said below
- return_cell: int32 [3, 32768], P(None, ('gx', 'gy', 'gz')), may hold values from -1 to 32767, as said below
- velocity: float32 [3, 32, 64, 512], P(None, 'gx', 'gy', 'gz'), may hold values from -6 to 6
Outputs:
- new_velocity: float32 [3, 32, 64, 512], P(None, 'gx', 'gy', 'gz')
- indicator: float32 [32, 64, 512], P('gx', 'gy', 'gz')
- vertex_velocity: float32 [9, 32768], P(None, ('gx', 'gy', 'gz'))
The draws below stay inside these ranges and needn't reach their ends.
Inputs may be any that keep to these rules, and one draw needn't show every extreme that they name: `send_index`: each row lists distinct local triangle indices of its owner in its first entries and -1 in the rest; every row has at least one triangle; an owner lists each of its triangles at most once over all its rows; for some bricks every owner fills all 128 slots. `near_index`: A value j * 128 + k names a slot that holds a triangle: k is below the number of triangles that owner j of the cell's row along gz lists for the cell's brick. `return_cell`: -1 where the vertex lies outside the brick. `tri_geom`: row 9 lies between 0.25 and 3.
All inputs are finite; a program needn't handle non-finite values.
Results may differ from the reference program's by a relative error of at most 0.0003.
Values sent between devices are 32-bit elements; how exact they have to be, the bound alone decides.
A program may use at most 128 MiB of HBM per device.

```python
import jax
import jax.numpy as jnp
from jax import lax

BX = 8
BY = 32
BZ = 128
CAP = 128
NSWEEP = 4
BRICKS_X = 4
BRICKS_Y = 2
BRICKS_Z = 4
GROUP = 8
BRICKS = 32
TRI_DEV = 1024
TRIS = 32768
SLOTS = 1024
CELLS = 32768
NX = 32
NY = 64
NZ = 512


def routing(key):
    key_hot, key_first, key_count = jax.random.split(jax.random.fold_in(key, 11), 3)
    is_hot = jax.random.randint(key_hot, (GROUP,), 0, 4) == 0
    first_hot = jax.random.randint(key_first, (), 0, GROUP)
    is_hot = is_hot | (jnp.arange(GROUP) == first_hot)
    counts = jnp.where(is_hot[None, :], CAP, jax.random.randint(key_count, (BRICKS, GROUP), 1, CAP + 1)).astype(jnp.int32)
    key_list = jax.random.split(jax.random.fold_in(key, 12), BRICKS)
    shuffled = jax.vmap(lambda subkey: jax.random.permutation(subkey, TRI_DEV))(key_list).astype(jnp.int32)
    offset = jnp.cumsum(counts, axis=1) - counts
    slot_ids = jnp.arange(CAP).astype(jnp.int32)
    position = offset[:, :, None] + slot_ids[None, None, :]
    filled = slot_ids[None, None, :] < counts[:, :, None]
    position = jnp.where(filled, position, 0)
    chosen = jnp.take_along_axis(shuffled, position.reshape(BRICKS, GROUP * CAP), axis=1).reshape(BRICKS, GROUP, CAP)
    return (counts, jnp.where(filled, chosen, -1).astype(jnp.int32))


def draw_send_index(key, part):
    counts, listed = routing(key)
    return listed.reshape(BRICKS * GROUP, CAP)


def draw_tri_geom(key, part):
    counts, listed = routing(key)
    rows = jnp.arange(BRICKS).astype(jnp.int32)[:, None, None]
    target = jnp.where(listed < 0, TRI_DEV, listed)
    dest_ids = jnp.broadcast_to(jnp.arange(GROUP).astype(jnp.int32)[None, :, None], listed.shape)
    dest = jnp.full((BRICKS, TRI_DEV + 1), -1, jnp.int32).at[rows, target].set(dest_ids)[:, :TRI_DEV]
    sent = dest >= 0
    safe_dest = jnp.maximum(dest, 0)
    row_z = (jnp.arange(BRICKS).astype(jnp.int32) % BRICKS_Z)[:, None]
    key_in, key_off, key_ten = jax.random.split(jax.random.fold_in(key, 13), 3)
    inside = jax.random.uniform(key_in, (3, BRICKS, TRI_DEV), jnp.float32)
    centre_x = jnp.where(sent, (safe_dest // BRICKS_Y * BX).astype(jnp.float32) + inside[0] * BX, inside[0] * NX)
    centre_y = jnp.where(sent, (safe_dest % BRICKS_Y * BY).astype(jnp.float32) + inside[1] * BY, inside[1] * NY)
    centre_z = jnp.where(sent, (row_z * BZ).astype(jnp.float32) + inside[2] * BZ, inside[2] * NZ)
    spread = 3.0
    tension = jnp.exp(jax.random.uniform(key_ten, (BRICKS, TRI_DEV), jnp.float32, jnp.log(0.5), jnp.log(2.0)))
    offsets = jax.random.normal(key_off, (9, BRICKS, TRI_DEV), jnp.float32) * spread
    centres = jnp.stack([centre_x, centre_y, centre_z] * 3)
    geometry = jnp.concatenate([centres + offsets, tension[None]], axis=0)
    return geometry.reshape(10, TRIS).astype(jnp.float32)


def draw_near_index(key, part):
    counts, listed = routing(key)
    grid_x = (jnp.arange(NX).astype(jnp.int32) // BX)[:, None, None]
    grid_y = (jnp.arange(NY).astype(jnp.int32) // BY)[None, :, None]
    grid_z = (jnp.arange(NZ).astype(jnp.int32) // BZ)[None, None, :]
    brick_row = grid_x * BRICKS_Y + grid_y
    key_src, key_slot = jax.random.split(jax.random.fold_in(key, 14))
    source = jax.random.randint(key_src, (NX, NY, NZ), 0, GROUP).astype(jnp.int32)
    owner = source * BRICKS_Z + grid_z
    limit = counts[owner, brick_row]
    within = jax.random.randint(key_slot, (NX, NY, NZ), 0, limit).astype(jnp.int32)
    return (source * CAP + within).astype(jnp.int32)


def draw_return_cell(key, part):
    key_out, key_cell = jax.random.split(jax.random.fold_in(key, 15))
    shape = (3, BRICKS * SLOTS)
    outside = jax.random.randint(key_out, shape, 0, 3) == 0
    return jnp.where(outside, -1, jax.random.randint(key_cell, shape, 0, CELLS)).astype(jnp.int32)


def shard_levels(own_key, extent, cuts, smallest, high):
    loudness, own = 1.0, jax.random.fold_in(own_key, 6)
    for axis_at, parts in cuts:
        steps = jnp.exp(jax.random.uniform(jax.random.fold_in(own, axis_at), (parts,), jnp.float32, smallest / len(cuts), high / len(cuts)))
        loudness = loudness * jnp.repeat(steps, extent[axis_at] // parts).reshape([-1 if axis == axis_at else 1 for axis in range(len(extent))])
    return loudness


def centred(own_key, extent, width, bound, cuts=(), dtype=jnp.bfloat16):
    gain = shard_levels(own_key, extent, cuts, -0.22, 0.18) if cuts else 1.0
    drawn = jax.random.normal(own_key, extent, jnp.float32) * width * gain
    return jnp.minimum(jnp.maximum(drawn, -bound), bound).astype(dtype)


def setup_inputs(seed: int = 0) -> dict:
    splits = jax.random.split(jax.random.key(seed), 6)
    tri_geom = draw_tri_geom(jax.random.fold_in(splits[5], 71), 0)
    send_index = draw_send_index(jax.random.fold_in(splits[5], 71), 0)
    near_index = draw_near_index(jax.random.fold_in(splits[5], 71), 0)
    return_cell = draw_return_cell(jax.random.fold_in(splits[5], 71), 0)
    velocity = centred(splits[4], (3, NX, NY, NZ), 1.0, 6.0, ((1, 4), (2, 2), (3, 4)), jnp.float32)
    return {"tri_geom": tri_geom, "send_index": send_index, "near_index": near_index, "return_cell": return_cell, "velocity": velocity}


time_step = 0.04
smear_width = 4.0
rho_liquid = 1.0
rho_gas = 0.05
mu_liquid = 2.0
mu_gas = 0.2

def brick_view(grid):
    leading = grid.shape[:-3]
    count = len(leading)
    shaped = grid.reshape(leading + (BRICKS_X, BX, BRICKS_Y, BY, BRICKS_Z, BZ))
    axes_order = tuple(range(count)) + (count, count + 2, count + 4, count + 1, count + 3, count + 5)
    return shaped.transpose(axes_order).reshape(leading + (BRICKS, CELLS))

def grid_view(blocks):
    leading = blocks.shape[:-2]
    count = len(leading)
    shaped = blocks.reshape(leading + (BRICKS_X, BRICKS_Y, BRICKS_Z, BX, BY, BZ))
    axes_order = tuple(range(count)) + (count, count + 3, count + 1, count + 4, count + 2, count + 5)
    return shaped.transpose(axes_order).reshape(leading + (NX, NY, NZ))

def slot_table(slots):
    first = slots[0:3]
    second = slots[3:6]
    third = slots[6:9]
    edge_one = second - first
    edge_two = third - first
    normal_x = edge_one[1] * edge_two[2] - edge_one[2] * edge_two[1]
    normal_y = edge_one[2] * edge_two[0] - edge_one[0] * edge_two[2]
    normal_z = edge_one[0] * edge_two[1] - edge_one[1] * edge_two[0]
    length = jnp.sqrt(normal_x * normal_x + normal_y * normal_y + normal_z * normal_z)
    scale = jnp.maximum(length, 1.0)
    centre = (first + second + third) / 3.0
    return jnp.stack([normal_x / scale, normal_y / scale, normal_z / scale, centre[0], centre[1], centre[2], slots[9]])

def reference(tri_geom, send_index, near_index, return_cell, velocity):
    owners = tri_geom.reshape(10, BRICKS, TRI_DEV)
    listed = send_index.reshape(BRICKS, GROUP * CAP)
    filled = listed >= 0
    gathered = jnp.take_along_axis(owners, jnp.maximum(listed, 0)[None], axis=2)
    gathered = jnp.where(filled[None], gathered, 0.0)
    received = gathered.reshape(10, GROUP, BRICKS_Z, GROUP, CAP).transpose(0, 3, 2, 1, 4).reshape(10, BRICKS, SLOTS)
    near_blocks = brick_view(near_index)
    brick_ids = jnp.arange(BRICKS).astype(jnp.int32)
    cell_ids = jnp.arange(CELLS).astype(jnp.int32)
    local_x = cell_ids // (BY * BZ)
    local_y = cell_ids // BZ % BY
    local_z = cell_ids % BZ

    def per_brick(packed):
        brick_id, slots, nearest = packed
        lookup = slot_table(slots)
        picked = jnp.take(lookup, nearest, axis=1)
        pos_x = (brick_id // (BRICKS_Y * BRICKS_Z) * BX + local_x).astype(jnp.float32) + 0.5
        pos_y = (brick_id // BRICKS_Z % BRICKS_Y * BY + local_y).astype(jnp.float32) + 0.5
        pos_z = (brick_id % BRICKS_Z * BZ + local_z).astype(jnp.float32) + 0.5
        distance = picked[0] * (pos_x - picked[3]) + picked[1] * (pos_y - picked[4]) + picked[2] * (pos_z - picked[5])
        return (0.5 * (1.0 + jnp.tanh(distance / smear_width)), picked[6])
    ind_blocks, ten_blocks = lax.map(per_brick, (brick_ids, received.transpose(1, 0, 2), near_blocks))
    indicator = grid_view(ind_blocks)
    tension = grid_view(ten_blocks)
    gradient = jnp.stack([(jnp.roll(indicator, -1, axis_id) - jnp.roll(indicator, 1, axis_id)) * 0.5 for axis_id in range(3)])
    density = rho_liquid + (rho_gas - rho_liquid) * indicator
    viscosity = mu_liquid + (mu_gas - mu_liquid) * indicator
    diffusion = viscosity / density
    forcing = tension * gradient / density
    current = velocity
    for repeat in range(NSWEEP):
        laplace = jnp.roll(current, -1, 1) + jnp.roll(current, 1, 1)
        laplace = laplace + jnp.roll(current, -1, 2) + jnp.roll(current, 1, 2)
        laplace = laplace + jnp.roll(current, -1, 3) + jnp.roll(current, 1, 3)
        laplace = laplace - 6.0 * current
        current = current + time_step * (diffusion * laplace + forcing)
    field_blocks = brick_view(current)
    cells_back = return_cell.reshape(3, BRICKS, SLOTS)
    samples = []
    for vertex in range(3):
        taken = jnp.take_along_axis(field_blocks, jnp.maximum(cells_back[vertex], 0)[None], axis=2)
        samples.append(jnp.where(cells_back[vertex][None] >= 0, taken, 0.0))
    sample = jnp.stack(samples, axis=1).reshape(9, BRICKS, SLOTS)
    back = sample.reshape(9, GROUP, BRICKS_Z, GROUP, CAP).transpose(0, 3, 2, 1, 4).reshape(9, BRICKS, GROUP * CAP)
    target = jnp.where(filled, listed, TRI_DEV)
    rows = jnp.arange(BRICKS).astype(jnp.int32)[:, None]
    vertex_velocity = jnp.zeros((9, BRICKS, TRI_DEV), jnp.float32).at[:, rows, target].add(back, mode='drop')
    return (current, indicator, vertex_velocity.reshape(9, TRIS))
```

```python
import jax
import jax.numpy as jnp
from jax import lax
from jax.experimental import pallas as pl
from jax.experimental.pallas import tpu as pltpu
from jax.sharding import PartitionSpec as P

CAP = 128
NSWEEP = 4
LANES = 128


time_step = 0.04
smear_width = 4.0
rho_liquid = 1.0
rho_gas = 0.05
mu_liquid = 2.0
mu_gas = 0.2


def loop(count, body, init):
    if count <= 8:
        for i in range(count):
            init = body(i, init)
        return init
    return lax.fori_loop(0, count, body, init)


def span(low, high, step, body, init):
    turns = (high - low) // step
    if turns > 1:

        def turn(i, carry):
            for k in range(step):
                carry = body(low + i * step + k, carry)
            return carry

        init = lax.fori_loop(0, turns, turn, init)
        low += turns * step
    for x in range(low, high):
        init = body(x, init)
    return init


UN_NEAR, UN_SWEEP, UN_FIRST, UN_FORCE, UN_INV = 2, 3, 4, 3, 4


def lane_pick(source, lane):
    return jnp.take_along_axis(source, lane, axis=1, mode="promise_in_bounds")


def build_table(tri_ref, table_ref):
    for t in range(table_ref.shape[0]):
        here = slice(t * LANES, (t + 1) * LANES)
        row = [tri_ref[i : i + 1, here] for i in range(10)]
        ax, ay, az = row[3] - row[0], row[4] - row[1], row[5] - row[2]
        bx, by, bz = row[6] - row[0], row[7] - row[1], row[8] - row[2]
        nx = ay * bz - az * by
        ny = az * bx - ax * bz
        nz = ax * by - ay * bx
        scale = jnp.maximum(jnp.sqrt(nx * nx + ny * ny + nz * nz), 1.0)
        table_ref[t, 0:1] = nx / scale
        table_ref[t, 1:2] = ny / scale
        table_ref[t, 2:3] = nz / scale
        for i in range(3):
            table_ref[t, 3 + i : 4 + i] = (row[i] + row[3 + i] + row[6 + i]) / 3.0
        table_ref[t, 6:7] = row[9]
        table_ref[t, 7:8] = row[9]


def pick_outgoing(send_ref, table_ref, out_ref):
    def each(d, carry):
        index = jnp.broadcast_to(send_ref[pl.ds(d, 1), :], (8, LANES))
        lane, tile = index & (LANES - 1), index >> 7

        def inner(t, found):
            return jnp.where(tile == t, lane_pick(table_ref[t], lane), found)

        out_ref[d] = loop(table_ref.shape[0], inner, jnp.zeros((8, LANES), jnp.float32))
        return carry

    loop(send_ref.shape[0], each, 0)


def local_table(arrived_ref, tab_ref, origin):
    nx, ny, nz = (arrived_ref[:, i, :] for i in range(3))
    offset = nx * (origin[0] - arrived_ref[:, 3, :])
    offset = offset + ny * (origin[1] - arrived_ref[:, 4, :])
    offset = offset + nz * (origin[2] - arrived_ref[:, 5, :])
    tab_ref[0], tab_ref[1], tab_ref[2] = nx, ny, nz
    tab_ref[3] = offset
    tab_ref[4] = arrived_ref[:, 6, :]


def iota(shape, axis):
    return lax.broadcasted_iota(jnp.int32, shape, axis)


def pack_lanes(plane, p, packed):
    here = (iota(plane.shape, 1) >> 1) == p
    return jnp.where(here, pltpu.roll(plane, 2 * p + 1, 1), packed)


def pack_rows(plane, c, x, row_ref):
    last = plane.shape[0] - 1
    row_ref[0, c, pl.ds(x, 1), :] = plane[0:1]
    row_ref[1, c, pl.ds(x, 1), :] = plane[last : last + 1]


def pack_faces(planes, x, row_ref, packed):
    size_x = row_ref.shape[2]
    for c, plane in enumerate(planes):
        pack_rows(plane, c, x, row_ref)
        packed = pack_lanes(plane, c * size_x + x, packed)
    return packed


def mix_lanes(halo_ref, mix_ref):
    even = (iota(mix_ref.shape, 1) & 1) == 0
    mix_ref[...] = jnp.where(even, halo_ref[0], halo_ref[1])


def around(field_ref, row_ref, mix_ref, c, x, p):
    size_y, size_z = field_ref.shape[2:]
    row, lane = iota((size_y, size_z), 0), iota((size_y, size_z), 1)
    mid = field_ref[c, x + 1]
    low_y = jnp.where(
        row == 0,
        jnp.broadcast_to(row_ref[0, c, pl.ds(x, 1), :], mid.shape),
        pltpu.roll(mid, 1, 0),
    )
    high_y = jnp.where(
        row == size_y - 1,
        jnp.broadcast_to(row_ref[1, c, pl.ds(x, 1), :], mid.shape),
        pltpu.roll(mid, size_y - 1, 0),
    )
    ends = pltpu.roll(mix_ref[...], size_z - 1 - 2 * p, 1)
    low_z = pltpu.roll(jnp.where(lane == size_z - 1, ends, mid), 1, 1)
    high_z = pltpu.roll(jnp.where(lane == 0, ends, mid), size_z - 1, 1)
    return mid, field_ref[c, x], field_ref[c, x + 2], low_y, high_y, low_z, high_z


def lookup(tab_ref, index):
    lane, owner = index & (LANES - 1), index >> 7

    def inner(j, found):
        here = owner == j
        return tuple(
            jnp.where(
                here,
                lane_pick(jnp.broadcast_to(tab_ref[f, pl.ds(j, 1), :], index.shape), lane),
                found[f],
            )
            for f in range(5)
        )

    zero = jnp.zeros(index.shape, jnp.float32)
    return loop(tab_ref.shape[1], inner, (zero,) * 5)


def nearest_plane(tab_ref, near_ref, ind_ref, ten_ref, x):
    size_y, size_z = near_ref.shape[1:]
    tall = 8 if tab_ref.shape[1] <= 8 else size_y
    pos_x = jnp.asarray(x).astype(jnp.float32) + 0.5
    pos_z = iota((tall, size_z), 1).astype(jnp.float32) + 0.5
    parts = []
    for r in range(0, size_y, tall):
        here = slice(r, r + tall)
        nx, ny, nz, offset, tension = lookup(tab_ref, near_ref[x, here, :])
        pos_y = iota((tall, size_z), 0).astype(jnp.float32) + (r + 0.5)
        distance = nx * pos_x + ny * pos_y + nz * pos_z + offset
        indicator = 0.5 * (1.0 + jnp.tanh(distance / smear_width))
        ind_ref[0, x + 1, here, :] = indicator
        ten_ref[x, here, :] = tension
        parts.append(indicator)
    return jnp.concatenate(parts, axis=0)


def material(ind_ref, ten_ref, diff_ref):
    def plane(x, carry):
        indicator = ind_ref[0, x + 1]
        density = rho_liquid + (rho_gas - rho_liquid) * indicator
        viscosity = mu_liquid + (mu_gas - mu_liquid) * indicator
        share = time_step / density
        diff_ref[x] = viscosity * share
        ten_ref[x] = ten_ref[x] * (0.5 * share)
        return carry

    span(0, ten_ref.shape[0], UN_FORCE, plane, 0)


def forces(ind_ref, row_ref, mix_ref, ten_ref, force_ref, x):
    near = around(ind_ref, row_ref, mix_ref, 0, x, x)
    for a in range(3):
        force_ref[a, x] = ten_ref[x] * (near[2 * a + 2] - near[2 * a + 1])


def advance(old_ref, row_ref, mix_ref, diff_ref, force_ref, new_ref, x):
    size_x = diff_ref.shape[0]
    diffusion = diff_ref[x]
    planes = []
    for c in range(3):
        mid, *near = around(old_ref, row_ref, mix_ref, c, x, c * size_x + x)
        laplace = near[0] + near[1] + near[2] + near[3] + near[4] + near[5] - 6.0 * mid
        planes.append(mid + (diffusion * laplace + force_ref[c, x]))
        new_ref[c, x + 1] = planes[-1]
    return planes


def row_onehot(cell_ref, hot_ref):
    rows, slots = hot_ref.shape[1:]

    def each(i, carry):
        here = pl.ds(pl.multiple_of(i * LANES, LANES), LANES)
        for v in range(3):
            row = jnp.broadcast_to(cell_ref[v : v + 1, here] >> 7, (rows, LANES))
            hit = iota((rows, LANES), 0) == row
            hot_ref[v, :, here] = jnp.where(hit, 1.0, 0.0).astype(jnp.bfloat16)
        return carry

    lax.fori_loop(0, slots // LANES, each, 0)


def sample_field(vel_ref, cell_ref, hot_ref, out_ref, send, first, step):
    rows, slots = hot_ref.shape[1:]
    size_x = vel_ref.shape[1] - 2
    parts = [vel_ref[c, 1 : size_x + 1].reshape(rows, LANES).T for c in range(3)]
    field = jnp.concatenate(parts, axis=0)
    high = field.astype(jnp.bfloat16)
    low = (field - high.astype(jnp.float32)).astype(jnp.bfloat16)
    width = 256
    turns = slots // width

    def each(k, carry):
        i = (first + k * step + turns) % turns
        here = pl.ds(pl.multiple_of(i * width, width), width)
        for v in range(3):
            hot = hot_ref[v, :, here]
            got = jnp.dot(high, hot, preferred_element_type=jnp.float32)
            got = got + jnp.dot(low, hot, preferred_element_type=jnp.float32)
            lane = jnp.broadcast_to(cell_ref[v : v + 1, here] & (LANES - 1), (LANES, width))
            hit = iota((LANES, width), 0) == lane
            for c in range(3):
                picked = jnp.where(hit, got[c * LANES : (c + 1) * LANES], 0.0)
                total = jnp.sum(picked, axis=0, keepdims=True)
                for k in range(width // LANES):
                    out_ref[i * (width // LANES) + k, 3 * c + v : 3 * c + v + 1] = total[
                        :, k * LANES : (k + 1) * LANES
                    ]
        for k in range(width // LANES):
            send(i * (width // LANES) + k)
        return carry

    lax.fori_loop(0, turns, each, 0)


def invert(send_ref, inv_ref):
    tiles = inv_ref.shape[0]
    lane = iota((LANES, LANES), 1)
    place = iota((LANES, LANES), 0)
    inv_ref[...] = jnp.full(inv_ref.shape, -1, jnp.int32)

    def each(d, carry):
        listed = jnp.broadcast_to(send_ref[pl.ds(d, 1), :], (LANES, LANES)).T
        slot = place + (d * LANES + 1)

        def inner(t, carry):
            hit = jnp.where(listed - t * LANES == lane, slot, 0)
            inv_ref[pl.ds(t, 1), :] += jnp.sum(hit, axis=0, keepdims=True)
            return carry

        loop(tiles, inner, 0)
        return carry

    span(0, send_ref.shape[0], UN_INV if send_ref.shape[0] <= 8 else 1, each, 0)


def place_back(inv_ref, back_ref, out_ref):
    tall = back_ref.shape[1]

    def each(t, carry):
        index = jnp.broadcast_to(inv_ref[pl.ds(t, 1), :], (tall, LANES))
        lane, dest = index & (LANES - 1), index >> 7

        def inner(d, found):
            return jnp.where(dest == d, lane_pick(back_ref[d], lane), found)

        found = loop(back_ref.shape[0], inner, jnp.zeros((tall, LANES), jnp.float32))
        start = t * LANES if isinstance(t, int) else pl.multiple_of(t * LANES, LANES)
        out_ref[:, pl.ds(start, LANES)] = found[:9]
        return carry

    loop(inv_ref.shape[0], each, 0)


def f32(*shape):
    return jax.ShapeDtypeStruct(shape, jnp.float32)


AXES = ("gx", "gy", "gz")


def flow_kernel(
    tri_hbm,
    send_hbm,
    near_hbm,
    cell_hbm,
    vel_hbm,
    vel_out,
    ind_out,
    back_out,
    inv_out,
    tri_ref,
    send_ref,
    near_ref,
    cell_ref,
    table_ref,
    out_ref,
    arrived_ref,
    tab_ref,
    ind_ref,
    ten_ref,
    diff_ref,
    force_ref,
    state_ref,
    ind_rows,
    ind_lanes,
    ind_row_halo,
    ind_lane_halo,
    rows_ref,
    lanes_ref,
    row_halo,
    lane_halo,
    mix_ref,
    hot_ref,
    inv_ref,
    sample_ref,
    back_ref,
    in_sem,
    out_sem,
    there_send,
    there_recv,
    back_send,
    back_recv,
    face_send,
    face_recv,
):
    size = {a: lax.axis_size(a) for a in AXES}
    at = {a: lax.axis_index(a) for a in AXES}
    count = size["gx"] * size["gy"]
    me = at["gx"] * size["gy"] + at["gy"]
    extent = near_ref.shape
    size_x = extent[0]

    def other(d):
        return {"gx": d // size["gy"], "gy": d % size["gy"]}

    def beside(axis, step):
        return {axis: (at[axis] + step + size[axis]) % size[axis]}

    def peers(body):
        if count <= 8:
            for r in range(1, count):
                body((me + r) % count)
        else:
            pl.loop(1, count)(lambda r: body((me + r) % count))

    loads = [
        pltpu.make_async_copy(src, dst, in_sem.at[i])
        for i, (src, dst) in enumerate(
            (
                (tri_hbm, tri_ref),
                (send_hbm, send_ref),
                (vel_hbm, state_ref.at[0, :, 1 : size_x + 1]),
                (near_hbm, near_ref),
                (cell_hbm, cell_ref),
            )
        )
    ]
    for load in loads:
        load.start()
    barrier = pltpu.get_barrier_semaphore()

    def greet(device):
        pl.semaphore_signal(
            barrier, inc=1, device_id=device, device_id_type=pl.DeviceIdType.MESH
        )

    peers(lambda d: greet(other(d)))
    greet(beside("gz", 1))
    greet(beside("gz", -1))

    def remote(src, dst, send_sem, recv_sem, device):
        return pltpu.make_async_remote_copy(
            src_ref=src,
            dst_ref=dst,
            send_sem=send_sem,
            recv_sem=recv_sem,
            device_id=device,
            device_id_type=pl.DeviceIdType.MESH,
        )

    def faces(n, field, rows, lanes, halo_rows, halo_lanes):
        pairs = (
            ("gx", 1, field.at[:, size_x], field.at[:, 0]),
            ("gx", -1, field.at[:, 1], field.at[:, size_x + 1]),
            ("gy", 1, rows.at[1], halo_rows.at[0]),
            ("gy", -1, rows.at[0], halo_rows.at[1]),
            ("gz", 1, lanes, halo_lanes.at[0]),
            ("gz", -1, lanes, halo_lanes.at[1]),
        )
        return [
            remote(src, dst, face_send.at[n, i], face_recv.at[n, i], beside(axis, step))
            for i, (axis, step, src, dst) in enumerate(pairs)
        ]

    rounds = [
        faces(
            n,
            state_ref.at[n],
            rows_ref.at[n],
            lanes_ref.at[n],
            row_halo.at[n],
            lane_halo.at[n],
        )
        for n in range(NSWEEP)
    ]
    ind_round = faces(NSWEEP, ind_ref, ind_rows, ind_lanes, ind_row_halo, ind_lane_halo)

    def there(src, dst):
        return remote(
            out_ref.at[dst], arrived_ref.at[src], there_send.at[dst], there_recv.at[src], other(dst)
        )

    def back(src, dst):
        return remote(
            sample_ref.at[dst], back_ref.at[src], back_send.at[dst], back_recv.at[src], other(dst)
        )

    loads[0].wait()
    loads[1].wait()
    build_table(tri_ref, table_ref)
    pick_outgoing(send_ref, table_ref, out_ref)
    pl.semaphore_wait(barrier, count + 1)
    peers(lambda d: there(me, d).start())
    arrived_ref[me] = out_ref[me]

    def start_x(copies):
        lowest = at["gx"] == 0
        pl.when(lowest)(lambda: copies[1].start())
        copies[0].start()
        pl.when(jnp.logical_not(lowest))(lambda: copies[1].start())

    edges = sorted({0, size_x - 1})
    zero = jnp.zeros(extent[1:], jnp.float32)

    def first_faces(x, packed):
        planes = [state_ref[0, c, x + 1] for c in range(3)]
        return pack_faces(planes, x, rows_ref.at[0], packed)

    loads[2].wait()
    lanes_ref[0] = span(0, size_x, UN_FIRST, first_faces, zero)
    loads[4].wait()
    row_onehot(cell_ref, hot_ref)
    start_x(rounds[0][:2])
    for copy in rounds[0][2:]:
        copy.start()
    invert(send_ref, inv_ref)
    put_inv = pltpu.make_async_copy(inv_ref, inv_out, out_sem.at[3])
    put_inv.start()
    loads[3].wait()
    peers(lambda d: there(d, me).wait_recv())
    origin = [(at[a] * n).astype(jnp.float32) for a, n in zip(AXES, extent)]
    local_table(arrived_ref, tab_ref, origin)

    def near_plane(x):
        return nearest_plane(tab_ref, near_ref, ind_ref, ten_ref, x)

    def near_middle(x, packed):
        return pack_faces([near_plane(x)], x, ind_rows, packed)

    planes = [near_plane(x) for x in edges]
    start_x(ind_round[:2])
    packed = zero
    for x, plane in zip(edges, planes):
        packed = pack_faces([plane], x, ind_rows, packed)
    ind_lanes[...] = span(1, size_x - 1, UN_NEAR, near_middle, packed)
    for copy in ind_round[2:]:
        copy.start()
    put_ind = pltpu.make_async_copy(ind_ref.at[0, 1 : size_x + 1], ind_out, out_sem.at[0])
    put_ind.start()
    material(ind_ref, ten_ref, diff_ref)

    def force_plane(x, carry):
        forces(ind_ref, ind_row_halo, mix_ref.at[NSWEEP], ten_ref, force_ref, x)
        return carry

    for copy in ind_round[2:]:
        copy.wait_recv()
    mix_lanes(ind_lane_halo, mix_ref.at[NSWEEP])
    span(1, size_x - 1, UN_FORCE, force_plane, 0)

    for n in range(NSWEEP):
        last = n == NSWEEP - 1

        def plane(x):
            return advance(
                state_ref.at[n],
                row_halo.at[n],
                mix_ref.at[n],
                diff_ref,
                force_ref,
                state_ref.at[n + 1],
                x,
            )

        def middle(x, packed):
            planes = plane(x)
            return packed if last else pack_faces(planes, x, rows_ref.at[n + 1], packed)

        for copy in rounds[n][2:]:
            copy.wait_recv()
        mix_lanes(lane_halo.at[n], mix_ref.at[n])
        packed = span(1, size_x - 1, UN_SWEEP, middle, zero)
        if n == 0:
            for copy in ind_round[:2]:
                copy.wait_recv()
            for x in edges:
                force_plane(x, 0)
        for copy in rounds[n][:2]:
            copy.wait_recv()
        planes = [plane(x) for x in edges]
        if not last:
            start_x(rounds[n + 1][:2])
            for x, group in zip(edges, planes):
                packed = pack_faces(group, x, rows_ref.at[n + 1], packed)
            lanes_ref[n + 1] = packed
            for copy in rounds[n + 1][2:]:
                copy.start()
    put_vel = pltpu.make_async_copy(
        state_ref.at[NSWEEP, :, 1 : size_x + 1], vel_out, out_sem.at[1]
    )
    put_vel.start()

    def send_back(d):
        @pl.when(d != me)
        def _():
            back(me, d).start()

    share = sample_ref.shape[0] // 2 // size["gx"]
    upper = (2 * at["gx"]) // size["gx"]
    first = (at["gx"] + upper) * share - (1 - upper)
    sample_field(
        state_ref.at[NSWEEP], cell_ref, hot_ref, sample_ref, send_back, first, 2 * upper - 1
    )
    back_ref[me] = sample_ref[me]
    peers(lambda d: back(d, me).wait_recv())
    put_back = pltpu.make_async_copy(back_ref, back_out, out_sem.at[2])
    put_back.start()
    peers(lambda d: there(me, d).wait_send())
    peers(lambda d: back(me, d).wait_send())
    for group in (ind_round, *rounds):
        for copy in group:
            copy.wait_send()
    put_ind.wait()
    put_vel.wait()
    put_back.wait()
    put_inv.wait()


def finish_kernel(
    vel_hbm, ind_hbm, back_ref, inv_ref, vel_out, ind_out, vert_out, vert_ref, sem
):
    give = [
        pltpu.make_async_copy(vel_hbm, vel_out, sem.at[0]),
        pltpu.make_async_copy(ind_hbm, ind_out, sem.at[1]),
        pltpu.make_async_copy(vert_ref, vert_out, sem.at[2]),
    ]
    give[0].start()
    give[1].start()
    place_back(inv_ref, back_ref, vert_ref)
    give[2].start()
    for copy in give:
        copy.wait()


def per_device(tri_geom, send_index, near_index, return_cell, velocity):
    count = lax.axis_size("gx") * lax.axis_size("gy")
    tri_dev = tri_geom.shape[1]
    tiles = tri_dev // LANES
    size_x, size_y, size_z = near_index.shape
    slots = return_cell.shape[1]

    def vm(*shape):
        return pltpu.VMEM(shape, jnp.float32)

    dma = pltpu.SemaphoreType.DMA
    anywhere = pl.BlockSpec(memory_space=pl.ANY)
    left = pl.pallas_call(
        flow_kernel,
        out_shape=(
            f32(*velocity.shape),
            f32(*near_index.shape),
            f32(count, 16, LANES),
            jax.ShapeDtypeStruct((tiles, LANES), jnp.int32),
        ),
        in_specs=[anywhere] * 5,
        out_specs=(anywhere,) * 4,
        scratch_shapes=[
            vm(*tri_geom.shape),
            pltpu.VMEM(send_index.shape, jnp.int32),
            pltpu.VMEM(near_index.shape, jnp.int32),
            pltpu.VMEM(return_cell.shape, jnp.int32),
            vm(tiles, 8, LANES),
            vm(count, 8, LANES),
            vm(count, 8, LANES),
            vm(5, count, LANES),
            vm(1, size_x + 2, size_y, size_z),
            vm(size_x, size_y, size_z),
            vm(size_x, size_y, size_z),
            vm(3, size_x, size_y, size_z),
            vm(NSWEEP + 1, 3, size_x + 2, size_y, size_z),
            vm(2, 1, size_x, size_z),
            vm(size_y, size_z),
            vm(2, 1, size_x, size_z),
            vm(2, size_y, size_z),
            vm(NSWEEP, 2, 3, size_x, size_z),
            vm(NSWEEP, size_y, size_z),
            vm(NSWEEP, 2, 3, size_x, size_z),
            vm(NSWEEP, 2, size_y, size_z),
            vm(NSWEEP + 1, size_y, size_z),
            pltpu.VMEM((3, size_x * size_y, slots), jnp.bfloat16),
            pltpu.VMEM((tiles, LANES), jnp.int32),
            vm(count, 16, LANES),
            vm(count, 16, LANES),
            dma((5,)),
            dma((4,)),
            dma((count,)),
            dma((count,)),
            dma((count,)),
            dma((count,)),
            dma((NSWEEP + 1, 6)),
            dma((NSWEEP + 1, 6)),
        ],
        compiler_params=pltpu.CompilerParams(collective_id=0, has_side_effects=True, vmem_limit_bytes=28 << 20),
        name="flow",
    )(*(pltpu.with_memory_space_constraint(x, pltpu.HBM) for x in (tri_geom, send_index, near_index, return_cell, velocity)))
    whole = pl.BlockSpec(memory_space=pltpu.VMEM)
    return pl.pallas_call(
        finish_kernel,
        out_shape=(f32(*velocity.shape), f32(*near_index.shape), f32(9, tri_dev)),
        in_specs=[anywhere, anywhere, whole, whole],
        out_specs=(anywhere,) * 3,
        scratch_shapes=[vm(9, tri_dev), dma((3,))],
        compiler_params=pltpu.CompilerParams(vmem_limit_bytes=8 << 20),
        name="finish",
    )(*left)


def solution(mesh):
    placed = (
        P(None, ("gx", "gy", "gz")),
        P(("gx", "gy", "gz"), None),
        P("gx", "gy", "gz"),
        P(None, ("gx", "gy", "gz")),
        P(None, "gx", "gy", "gz"),
    )
    return jax.shard_map(
        per_device,
        mesh=mesh,
        in_specs=placed,
        out_specs=(P(None, "gx", "gy", "gz"), P("gx", "gy", "gz"), P(None, ("gx", "gy", "gz"))),
        check_vma=False,
    )
```

```python
import jax
import jax.numpy as jnp
from jax import lax
from jax.experimental import pallas as pl
from jax.experimental.pallas import tpu as pltpu
from jax.sharding import PartitionSpec as P

CAP = 128
NSWEEP = 4
LANES = 128


time_step = 0.04
smear_width = 4.0
rho_liquid = 1.0
rho_gas = 0.05
mu_liquid = 2.0
mu_gas = 0.2


def loop(count, body, init):
    if count <= 8:
        for i in range(count):
            init = body(i, init)
        return init
    return lax.fori_loop(0, count, body, init)


def span(low, high, step, body, init):
    turns = (high - low) // step
    if turns > 1:

        def turn(i, carry):
            for k in range(step):
                carry = body(low + i * step + k, carry)
            return carry

        init = lax.fori_loop(0, turns, turn, init)
        low += turns * step
    for x in range(low, high):
        init = body(x, init)
    return init


UN_NEAR, UN_SWEEP, UN_FIRST, UN_FORCE, UN_INV = 2, 3, 4, 3, 4


def lane_pick(source, lane):
    return jnp.take_along_axis(source, lane, axis=1, mode="promise_in_bounds")


def build_table(tri_ref, table_ref):
    for t in range(table_ref.shape[0]):
        here = slice(t * LANES, (t + 1) * LANES)
        row = [tri_ref[i : i + 1, here] for i in range(10)]
        ax, ay, az = row[3] - row[0], row[4] - row[1], row[5] - row[2]
        bx, by, bz = row[6] - row[0], row[7] - row[1], row[8] - row[2]
        nx = ay * bz - az * by
        ny = az * bx - ax * bz
        nz = ax * by - ay * bx
        scale = jnp.maximum(jnp.sqrt(nx * nx + ny * ny + nz * nz), 1.0)
        table_ref[t, 0:1] = nx / scale
        table_ref[t, 1:2] = ny / scale
        table_ref[t, 2:3] = nz / scale
        for i in range(3):
            table_ref[t, 3 + i : 4 + i] = (row[i] + row[3 + i] + row[6 + i]) / 3.0
        table_ref[t, 6:7] = row[9]
        table_ref[t, 7:8] = row[9]


def pick_outgoing(send_ref, table_ref, out_ref):
    def each(d, carry):
        index = jnp.broadcast_to(send_ref[pl.ds(d, 1), :], (8, LANES))
        lane, tile = index & (LANES - 1), index >> 7

        def inner(t, found):
            return jnp.where(tile == t, lane_pick(table_ref[t], lane), found)

        out_ref[d] = loop(table_ref.shape[0], inner, jnp.zeros((8, LANES), jnp.float32))
        return carry

    loop(send_ref.shape[0], each, 0)


def local_table(arrived_ref, tab_ref, origin):
    nx, ny, nz = (arrived_ref[:, i, :] for i in range(3))
    offset = nx * (origin[0] - arrived_ref[:, 3, :])
    offset = offset + ny * (origin[1] - arrived_ref[:, 4, :])
    offset = offset + nz * (origin[2] - arrived_ref[:, 5, :])
    tab_ref[0], tab_ref[1], tab_ref[2] = nx, ny, nz
    tab_ref[3] = offset
    tab_ref[4] = arrived_ref[:, 6, :]


def iota(shape, axis):
    return lax.broadcasted_iota(jnp.int32, shape, axis)


def pack_lanes(plane, p, packed):
    here = (iota(plane.shape, 1) >> 1) == p
    return jnp.where(here, pltpu.roll(plane, 2 * p + 1, 1), packed)


def pack_rows(plane, c, x, row_ref):
    last = plane.shape[0] - 1
    row_ref[0, c, pl.ds(x, 1), :] = plane[0:1]
    row_ref[1, c, pl.ds(x, 1), :] = plane[last : last + 1]


def pack_faces(planes, x, row_ref, packed):
    size_x = row_ref.shape[2]
    for c, plane in enumerate(planes):
        pack_rows(plane, c, x, row_ref)
        packed = pack_lanes(plane, c * size_x + x, packed)
    return packed


def mix_lanes(halo_ref, mix_ref):
    even = (iota(mix_ref.shape, 1) & 1) == 0
    mix_ref[...] = jnp.where(even, halo_ref[0], halo_ref[1])


def around(field_ref, row_ref, mix_ref, c, x, p):
    size_y, size_z = field_ref.shape[2:]
    row, lane = iota((size_y, size_z), 0), iota((size_y, size_z), 1)
    mid = field_ref[c, x + 1]
    low_y = jnp.where(
        row == 0,
        jnp.broadcast_to(row_ref[0, c, pl.ds(x, 1), :], mid.shape),
        pltpu.roll(mid, 1, 0),
    )
    high_y = jnp.where(
        row == size_y - 1,
        jnp.broadcast_to(row_ref[1, c, pl.ds(x, 1), :], mid.shape),
        pltpu.roll(mid, size_y - 1, 0),
    )
    ends = pltpu.roll(mix_ref[...], size_z - 1 - 2 * p, 1)
    low_z = pltpu.roll(jnp.where(lane == size_z - 1, ends, mid), 1, 1)
    high_z = pltpu.roll(jnp.where(lane == 0, ends, mid), size_z - 1, 1)
    return mid, field_ref[c, x], field_ref[c, x + 2], low_y, high_y, low_z, high_z


def lookup(tab_ref, index):
    lane, owner = index & (LANES - 1), index >> 7

    def inner(j, found):
        here = owner == j
        return tuple(
            jnp.where(
                here,
                lane_pick(jnp.broadcast_to(tab_ref[f, pl.ds(j, 1), :], index.shape), lane),
                found[f],
            )
            for f in range(5)
        )

    zero = jnp.zeros(index.shape, jnp.float32)
    return loop(tab_ref.shape[1], inner, (zero,) * 5)


def indicate(tab_ref, index, position):
    nx, ny, nz, offset, tension = lookup(tab_ref, index)
    pos_x, pos_y, pos_z = (jnp.asarray(p).astype(jnp.float32) + 0.5 for p in position)
    distance = nx * pos_x + ny * pos_y + nz * pos_z + offset
    return 0.5 * (1.0 + jnp.tanh(distance / smear_width)), tension


def nearest_plane(tab_ref, near_ref, ind_ref, ten_ref, x):
    size_y, size_z = near_ref.shape[1:]
    tall = 8 if tab_ref.shape[1] <= 8 else size_y
    for r in range(0, size_y, tall):
        here = slice(r, r + tall)
        position = (x, iota((tall, size_z), 0) + r, iota((tall, size_z), 1))
        indicator, tension = indicate(tab_ref, near_ref[x, here, :], position)
        ind_ref[0, x + 1, here, :] = indicator
        ten_ref[x, here, :] = tension


def nearest_faces(tab_ref, near_rows, near_lanes, row_ref, lane_ref):
    size_x, size_z = near_rows.shape[2:]
    size_y = near_lanes.shape[0]
    shape = (size_x, size_z)
    for side, y in ((0, 0), (1, size_y - 1)):
        position = (iota(shape, 0), y, iota(shape, 1))
        row_ref[side, 0] = indicate(tab_ref, near_rows[side, 0], position)[0]
    tall = 8 if tab_ref.shape[1] <= 8 else size_y
    for r in range(0, size_y, tall):
        here = slice(r, r + tall)
        lane = iota((tall, size_z), 1)
        position = (lane >> 1, iota((tall, size_z), 0) + r, (1 - (lane & 1)) * (size_z - 1))
        lane_ref[here, :] = indicate(tab_ref, near_lanes[here, :], position)[0]


def material(ind_ref, ten_ref, diff_ref):
    def plane(x, carry):
        indicator = ind_ref[0, x + 1]
        density = rho_liquid + (rho_gas - rho_liquid) * indicator
        viscosity = mu_liquid + (mu_gas - mu_liquid) * indicator
        share = time_step / density
        diff_ref[x] = viscosity * share
        ten_ref[x] = ten_ref[x] * (0.5 * share)
        return carry

    span(0, ten_ref.shape[0], UN_FORCE, plane, 0)


def forces(ind_ref, row_ref, mix_ref, ten_ref, force_ref, x):
    near = around(ind_ref, row_ref, mix_ref, 0, x, x)
    for a in range(3):
        force_ref[a, x] = ten_ref[x] * (near[2 * a + 2] - near[2 * a + 1])


def laplacian(old_ref, row_ref, mix_ref, c, x, p):
    mid, *near = around(old_ref, row_ref, mix_ref, c, x, p)
    return mid, near[0] + near[1] + near[2] + near[3] + near[4] + near[5] - 6.0 * mid


def advance(old_ref, row_ref, mix_ref, diff_ref, force_ref, new_ref, x):
    size_x = diff_ref.shape[0]
    diffusion = diff_ref[x]
    planes = []
    for c in range(3):
        mid, laplace = laplacian(old_ref, row_ref, mix_ref, c, x, c * size_x + x)
        planes.append(mid + (diffusion * laplace + force_ref[c, x]))
        new_ref[c, x + 1] = planes[-1]
    return planes


def advance_first(old_ref, diff_ref, force_ref, new_ref, x):
    diffusion = diff_ref[x]
    planes = []
    for c in range(3):
        planes.append(old_ref[c, x + 1] + (diffusion * new_ref[c, x + 1] + force_ref[c, x]))
        new_ref[c, x + 1] = planes[-1]
    return planes


def row_onehot(cell_ref, hot_ref):
    rows, slots = hot_ref.shape[1:]

    def each(i, carry):
        here = pl.ds(pl.multiple_of(i * LANES, LANES), LANES)
        for v in range(3):
            row = jnp.broadcast_to(cell_ref[v : v + 1, here] >> 7, (rows, LANES))
            hit = iota((rows, LANES), 0) == row
            hot_ref[v, :, here] = jnp.where(hit, 1.0, 0.0).astype(jnp.bfloat16)
        return carry

    lax.fori_loop(0, slots // LANES, each, 0)


def sample_field(vel_ref, cell_ref, hot_ref, out_ref, send, first, step):
    rows, slots = hot_ref.shape[1:]
    size_x = vel_ref.shape[1] - 2
    parts = [vel_ref[c, 1 : size_x + 1].reshape(rows, LANES).T for c in range(3)]
    field = jnp.concatenate(parts, axis=0)
    high = field.astype(jnp.bfloat16)
    low = (field - high.astype(jnp.float32)).astype(jnp.bfloat16)
    width = 256
    turns = slots // width

    def each(k, carry):
        i = (first + k * step + turns) % turns
        here = pl.ds(pl.multiple_of(i * width, width), width)
        for v in range(3):
            hot = hot_ref[v, :, here]
            got = jnp.dot(high, hot, preferred_element_type=jnp.float32)
            got = got + jnp.dot(low, hot, preferred_element_type=jnp.float32)
            lane = jnp.broadcast_to(cell_ref[v : v + 1, here] & (LANES - 1), (LANES, width))
            hit = iota((LANES, width), 0) == lane
            for c in range(3):
                picked = jnp.where(hit, got[c * LANES : (c + 1) * LANES], 0.0)
                total = jnp.sum(picked, axis=0, keepdims=True)
                for k in range(width // LANES):
                    out_ref[i * (width // LANES) + k, 3 * c + v : 3 * c + v + 1] = total[
                        :, k * LANES : (k + 1) * LANES
                    ]
        for k in range(width // LANES):
            send(i * (width // LANES) + k)
        return carry

    lax.fori_loop(0, turns, each, 0)


def invert(send_ref, inv_ref):
    tiles = inv_ref.shape[0]
    lane = iota((LANES, LANES), 1)
    place = iota((LANES, LANES), 0)
    inv_ref[...] = jnp.full(inv_ref.shape, -1, jnp.int32)

    def each(d, carry):
        listed = jnp.broadcast_to(send_ref[pl.ds(d, 1), :], (LANES, LANES)).T
        slot = place + (d * LANES + 1)

        def inner(t, carry):
            hit = jnp.where(listed - t * LANES == lane, slot, 0)
            inv_ref[pl.ds(t, 1), :] += jnp.sum(hit, axis=0, keepdims=True)
            return carry

        loop(tiles, inner, 0)
        return carry

    span(0, send_ref.shape[0], UN_INV if send_ref.shape[0] <= 8 else 1, each, 0)


def place_back(inv_ref, back_ref, d, out_ref):
    tall = back_ref.shape[1]

    def each(t, carry):
        index = jnp.broadcast_to(inv_ref[pl.ds(t, 1), :], (tall, LANES))
        lane, dest = index & (LANES - 1), index >> 7
        out_ref[t] = jnp.where(dest == d, lane_pick(back_ref[d], lane), out_ref[t])
        return carry

    loop(inv_ref.shape[0], each, 0)


def f32(*shape):
    return jax.ShapeDtypeStruct(shape, jnp.float32)


AXES = ("gx", "gy", "gz")


def flow_kernel(
    tri_hbm,
    send_hbm,
    near_hbm,
    cell_hbm,
    vel_hbm,
    vel_out,
    ind_out,
    vert_out,
    tri_ref,
    send_ref,
    near_ref,
    cell_ref,
    table_ref,
    out_ref,
    arrived_ref,
    tab_ref,
    ind_ref,
    ten_ref,
    diff_ref,
    force_ref,
    state_ref,
    ind_rows,
    ind_lanes,
    ind_row_halo,
    ind_lane_halo,
    rows_ref,
    lanes_ref,
    row_halo,
    lane_halo,
    mix_ref,
    near_rows,
    near_lanes,
    hot_ref,
    inv_ref,
    sample_ref,
    back_ref,
    vert_ref,
    in_sem,
    out_sem,
    there_send,
    there_recv,
    back_send,
    back_recv,
    face_send,
    face_recv,
):
    size = {a: lax.axis_size(a) for a in AXES}
    at = {a: lax.axis_index(a) for a in AXES}
    count = size["gx"] * size["gy"]
    me = at["gx"] * size["gy"] + at["gy"]
    extent = near_ref.shape
    size_x = extent[0]

    def other(d):
        return {"gx": d // size["gy"], "gy": d % size["gy"]}

    def beside(axis, step):
        return {axis: (at[axis] + step + size[axis]) % size[axis]}

    def peers(body):
        if count <= 8:
            for r in range(1, count):
                body((me + r) % count)
        else:
            pl.loop(1, count)(lambda r: body((me + r) % count))

    loads = [
        pltpu.make_async_copy(src, dst, in_sem.at[i])
        for i, (src, dst) in enumerate(
            (
                (tri_hbm, tri_ref),
                (send_hbm, send_ref),
                (vel_hbm, state_ref.at[0, :, 1 : size_x + 1]),
                (near_hbm, near_ref),
                (cell_hbm, cell_ref),
            )
        )
    ]
    for load in loads:
        load.start()
    barrier = pltpu.get_barrier_semaphore()

    def greet(device):
        pl.semaphore_signal(
            barrier, inc=1, device_id=device, device_id_type=pl.DeviceIdType.MESH
        )

    peers(lambda d: greet(other(d)))
    greet(beside("gz", 1))
    greet(beside("gz", -1))

    def remote(src, dst, send_sem, recv_sem, device):
        return pltpu.make_async_remote_copy(
            src_ref=src,
            dst_ref=dst,
            send_sem=send_sem,
            recv_sem=recv_sem,
            device_id=device,
            device_id_type=pl.DeviceIdType.MESH,
        )

    def faces(n, field, rows, lanes, halo_rows, halo_lanes):
        pairs = (
            ("gy", 1, rows.at[1], halo_rows.at[0]),
            ("gy", -1, rows.at[0], halo_rows.at[1]),
            ("gz", 1, lanes, halo_lanes.at[0]),
            ("gz", -1, lanes, halo_lanes.at[1]),
        )
        return [
            remote(src, dst, face_send.at[n, i], face_recv.at[n, i], beside(axis, step))
            for i, (axis, step, src, dst) in enumerate(pairs, 2)
        ]

    rounds = [
        faces(
            n,
            state_ref.at[n],
            rows_ref.at[n],
            lanes_ref.at[n],
            row_halo.at[n],
            lane_halo.at[n],
        )
        for n in range(NSWEEP)
    ]
    ind_round = faces(NSWEEP, ind_ref, ind_rows, ind_lanes, ind_row_halo, ind_lane_halo)

    def x_face(n, up):
        field = ind_ref if n == NSWEEP else state_ref.at[n]
        return remote(
            field.at[:, 1 + up * (size_x - 1)],
            field.at[:, (1 - up) * (size_x + 1)],
            face_send.at[n, 1 - up],
            face_recv.at[n, 1 - up],
            beside("gx", 2 * up - 1),
        )

    def there(src, dst):
        return remote(
            out_ref.at[dst], arrived_ref.at[src], there_send.at[dst], there_recv.at[src], other(dst)
        )

    def back(src, dst):
        return remote(
            sample_ref.at[dst], back_ref.at[src], back_send.at[dst], back_recv.at[src], other(dst)
        )

    loads[0].wait()
    loads[1].wait()
    build_table(tri_ref, table_ref)
    pick_outgoing(send_ref, table_ref, out_ref)
    pl.semaphore_wait(barrier, count + 1)
    peers(lambda d: there(me, d).start())
    arrived_ref[me] = out_ref[me]

    lowest = (size["gx"] - 1 - at["gx"]) // (size["gx"] - 1)
    sides = ((1 - lowest), lowest)
    zero = jnp.zeros(extent[1:], jnp.float32)

    def first_faces(x, packed):
        planes = [state_ref[0, c, x + 1] for c in range(3)]
        return pack_faces(planes, x, rows_ref.at[0], packed)

    def near_faces(x, packed):
        return pack_faces([near_ref[x]], x, near_rows, packed)

    loads[2].wait()
    lanes_ref[0] = span(0, size_x, UN_FIRST, first_faces, zero)
    loads[4].wait()
    row_onehot(cell_ref, hot_ref)
    for up in (0, 1):
        x_face(0, up).start()
    for copy in rounds[0]:
        copy.start()
    loads[3].wait()
    near_lanes[...] = span(0, size_x, UN_FIRST, near_faces, jnp.zeros(extent[1:], jnp.int32))
    invert(send_ref, inv_ref)
    vert_ref[...] = jnp.zeros(vert_ref.shape, jnp.float32)
    peers(lambda d: there(d, me).wait_recv())
    origin = [(at[a] * n).astype(jnp.float32) for a, n in zip(AXES, extent)]
    local_table(arrived_ref, tab_ref, origin)

    def near_plane(x, carry):
        nearest_plane(tab_ref, near_ref, ind_ref, ten_ref, x)
        return carry

    for up in sides:
        near_plane(up * (size_x - 1), 0)
        x_face(NSWEEP, up).start()
    nearest_faces(tab_ref, near_rows, near_lanes, ind_rows, ind_lanes)
    for copy in ind_round:
        copy.start()
    span(1, size_x - 1, UN_NEAR, near_plane, 0)
    put_ind = pltpu.make_async_copy(ind_ref.at[0, 1 : size_x + 1], ind_out, out_sem.at[0])
    put_ind.start()
    material(ind_ref, ten_ref, diff_ref)
    for up in (0, 1):
        x_face(0, up).wait_recv()
    for copy in rounds[0]:
        copy.wait_recv()
    mix_lanes(lane_halo.at[0], mix_ref.at[0])

    def first_laplacian(x, carry):
        for c in range(3):
            state_ref[1, c, x + 1] = laplacian(
                state_ref.at[0], row_halo.at[0], mix_ref.at[0], c, x, c * size_x + x
            )[1]
        return carry

    span(0, size_x, UN_FIRST, first_laplacian, 0)

    for n in range(NSWEEP):
        last = n == NSWEEP - 1
        faces_in = ind_round if n == 0 else rounds[n]

        def plane(x):
            if n == 0:
                forces(ind_ref, ind_row_halo, mix_ref.at[NSWEEP], ten_ref, force_ref, x)
                return advance_first(
                    state_ref.at[0], diff_ref, force_ref, state_ref.at[1], x
                )
            return advance(
                state_ref.at[n],
                row_halo.at[n],
                mix_ref.at[n],
                diff_ref,
                force_ref,
                state_ref.at[n + 1],
                x,
            )

        def middle(x, packed):
            planes = plane(x)
            return packed if last else pack_faces(planes, x, rows_ref.at[n + 1], packed)

        for copy in faces_in:
            copy.wait_recv()
        if n == 0:
            mix_lanes(ind_lane_halo, mix_ref.at[NSWEEP])
        else:
            mix_lanes(lane_halo.at[n], mix_ref.at[n])
        packed = span(1, size_x - 1, UN_SWEEP, middle, zero)
        edges = []
        for up in reversed(sides):
            x_face(n if n else NSWEEP, 1 - up).wait_recv()
            edges.append((up * (size_x - 1), plane(up * (size_x - 1))))
            if not last:
                x_face(n + 1, up).start()
        if not last:
            for x, planes in edges:
                packed = pack_faces(planes, x, rows_ref.at[n + 1], packed)
            lanes_ref[n + 1] = packed
            for copy in rounds[n + 1]:
                copy.start()
    put_vel = pltpu.make_async_copy(
        state_ref.at[NSWEEP, :, 1 : size_x + 1], vel_out, out_sem.at[1]
    )
    put_vel.start()

    def send_back(d):
        @pl.when(d != me)
        def _():
            back(me, d).start()

    share = sample_ref.shape[0] // 2 // size["gx"]
    upper = (2 * at["gx"]) // size["gx"]
    first = (at["gx"] + upper) * share - (1 - upper)
    sample_field(
        state_ref.at[NSWEEP], cell_ref, hot_ref, sample_ref, send_back, first, 2 * upper - 1
    )
    back_ref[me] = sample_ref[me]
    place_back(inv_ref, back_ref, me, vert_ref)

    def collect(d):
        back(d, me).wait_recv()
        place_back(inv_ref, back_ref, d, vert_ref)

    peers(collect)
    put_vert = pltpu.make_async_copy(vert_ref, vert_out, out_sem.at[2])
    put_vert.start()
    peers(lambda d: there(me, d).wait_send())
    peers(lambda d: back(me, d).wait_send())
    for n in range(NSWEEP + 1):
        for up in (0, 1):
            x_face(n, up).wait_send()
    for group in (ind_round, *rounds):
        for copy in group:
            copy.wait_send()
    put_ind.wait()
    put_vel.wait()
    put_vert.wait()


def finish_kernel(vel_hbm, ind_hbm, vert_ref, vel_out, ind_out, vert_out, flat_ref, sem):
    for t in range(vert_ref.shape[0]):
        flat_ref[:, t * LANES : (t + 1) * LANES] = vert_ref[t, :9]
    give = [
        pltpu.make_async_copy(vel_hbm, vel_out, sem.at[0]),
        pltpu.make_async_copy(ind_hbm, ind_out, sem.at[1]),
        pltpu.make_async_copy(flat_ref, vert_out, sem.at[2]),
    ]
    for copy in give:
        copy.start()
    for copy in give:
        copy.wait()


def per_device(tri_geom, send_index, near_index, return_cell, velocity):
    count = lax.axis_size("gx") * lax.axis_size("gy")
    tri_dev = tri_geom.shape[1]
    tiles = tri_dev // LANES
    size_x, size_y, size_z = near_index.shape
    slots = return_cell.shape[1]

    def vm(*shape):
        return pltpu.VMEM(shape, jnp.float32)

    dma = pltpu.SemaphoreType.DMA
    anywhere = pl.BlockSpec(memory_space=pl.ANY)
    left = pl.pallas_call(
        flow_kernel,
        out_shape=(
            f32(*velocity.shape),
            f32(*near_index.shape),
            f32(tiles, 16, LANES),
        ),
        in_specs=[anywhere] * 5,
        out_specs=(anywhere,) * 3,
        scratch_shapes=[
            vm(*tri_geom.shape),
            pltpu.VMEM(send_index.shape, jnp.int32),
            pltpu.VMEM(near_index.shape, jnp.int32),
            pltpu.VMEM(return_cell.shape, jnp.int32),
            vm(tiles, 8, LANES),
            vm(count, 8, LANES),
            vm(count, 8, LANES),
            vm(5, count, LANES),
            vm(1, size_x + 2, size_y, size_z),
            vm(size_x, size_y, size_z),
            vm(size_x, size_y, size_z),
            vm(3, size_x, size_y, size_z),
            vm(NSWEEP + 1, 3, size_x + 2, size_y, size_z),
            vm(2, 1, size_x, size_z),
            vm(size_y, size_z),
            vm(2, 1, size_x, size_z),
            vm(2, size_y, size_z),
            vm(NSWEEP, 2, 3, size_x, size_z),
            vm(NSWEEP, size_y, size_z),
            vm(NSWEEP, 2, 3, size_x, size_z),
            vm(NSWEEP, 2, size_y, size_z),
            vm(NSWEEP + 1, size_y, size_z),
            pltpu.VMEM((2, 1, size_x, size_z), jnp.int32),
            pltpu.VMEM((size_y, size_z), jnp.int32),
            pltpu.VMEM((3, size_x * size_y, slots), jnp.bfloat16),
            pltpu.VMEM((tiles, LANES), jnp.int32),
            vm(count, 16, LANES),
            vm(count, 16, LANES),
            vm(tiles, 16, LANES),
            dma((5,)),
            dma((3,)),
            dma((count,)),
            dma((count,)),
            dma((count,)),
            dma((count,)),
            dma((NSWEEP + 1, 6)),
            dma((NSWEEP + 1, 6)),
        ],
        compiler_params=pltpu.CompilerParams(collective_id=0, has_side_effects=True, vmem_limit_bytes=28 << 20),
        name="flow",
    )(*(pltpu.with_memory_space_constraint(x, pltpu.HBM) for x in (tri_geom, send_index, near_index, return_cell, velocity)))
    whole = pl.BlockSpec(memory_space=pltpu.VMEM)
    return pl.pallas_call(
        finish_kernel,
        out_shape=(f32(*velocity.shape), f32(*near_index.shape), f32(9, tri_dev)),
        in_specs=[anywhere, anywhere, whole],
        out_specs=(anywhere,) * 3,
        scratch_shapes=[vm(9, tri_dev), dma((3,))],
        compiler_params=pltpu.CompilerParams(vmem_limit_bytes=8 << 20),
        name="finish",
    )(*left)


def solution(mesh):
    placed = (
        P(None, ("gx", "gy", "gz")),
        P(("gx", "gy", "gz"), None),
        P("gx", "gy", "gz"),
        P(None, ("gx", "gy", "gz")),
        P(None, "gx", "gy", "gz"),
    )
    return jax.shard_map(
        per_device,
        mesh=mesh,
        in_specs=placed,
        out_specs=(P(None, "gx", "gy", "gz"), P("gx", "gy", "gz"), P(None, ("gx", "gy", "gz"))),
        check_vma=False,
    )
```

```python
import jax
import jax.numpy as jnp
from jax import lax
from jax.experimental import pallas as pl
from jax.experimental.pallas import tpu as pltpu
from jax.sharding import PartitionSpec as P

CAP = 128
NSWEEP = 4
LANES = 128


time_step = 0.04
smear_width = 4.0
rho_liquid = 1.0
rho_gas = 0.05
mu_liquid = 2.0
mu_gas = 0.2


def loop(count, body, init):
    if count <= 8:
        for i in range(count):
            init = body(i, init)
        return init
    return lax.fori_loop(0, count, body, init)


def span(low, high, step, body, init):
    turns = (high - low) // step
    if turns > 1:

        def turn(i, carry):
            for k in range(step):
                carry = body(low + i * step + k, carry)
            return carry

        init = lax.fori_loop(0, turns, turn, init)
        low += turns * step
    for x in range(low, high):
        init = body(x, init)
    return init


UN_NEAR, UN_SWEEP, UN_FIRST, UN_FORCE, UN_INV = 2, 3, 4, 3, 4


def lane_pick(source, lane):
    return jnp.take_along_axis(source, lane, axis=1, mode="promise_in_bounds")


def build_table(tri_ref, table_ref):
    for t in range(table_ref.shape[0]):
        here = slice(t * LANES, (t + 1) * LANES)
        row = [tri_ref[i : i + 1, here] for i in range(10)]
        ax, ay, az = row[3] - row[0], row[4] - row[1], row[5] - row[2]
        bx, by, bz = row[6] - row[0], row[7] - row[1], row[8] - row[2]
        nx = ay * bz - az * by
        ny = az * bx - ax * bz
        nz = ax * by - ay * bx
        scale = jnp.maximum(jnp.sqrt(nx * nx + ny * ny + nz * nz), 1.0)
        table_ref[t, 0:1] = nx / scale
        table_ref[t, 1:2] = ny / scale
        table_ref[t, 2:3] = nz / scale
        for i in range(3):
            table_ref[t, 3 + i : 4 + i] = (row[i] + row[3 + i] + row[6 + i]) / 3.0
        table_ref[t, 6:7] = row[9]
        table_ref[t, 7:8] = row[9]


def pick_outgoing(send_ref, table_ref, out_ref):
    def each(d, carry):
        index = jnp.broadcast_to(send_ref[pl.ds(d, 1), :], (8, LANES))
        lane, tile = index & (LANES - 1), index >> 7

        def inner(t, found):
            return jnp.where(tile == t, lane_pick(table_ref[t], lane), found)

        out_ref[d] = loop(table_ref.shape[0], inner, jnp.zeros((8, LANES), jnp.float32))
        return carry

    loop(send_ref.shape[0], each, 0)


def local_table(arrived_ref, tab_ref, origin):
    nx, ny, nz = (arrived_ref[:, i, :] for i in range(3))
    offset = nx * (origin[0] - arrived_ref[:, 3, :])
    offset = offset + ny * (origin[1] - arrived_ref[:, 4, :])
    offset = offset + nz * (origin[2] - arrived_ref[:, 5, :])
    tab_ref[0], tab_ref[1], tab_ref[2] = nx, ny, nz
    tab_ref[3] = offset
    tab_ref[4] = arrived_ref[:, 6, :]


def iota(shape, axis):
    return lax.broadcasted_iota(jnp.int32, shape, axis)


def pack_lanes(plane, p, packed):
    here = (iota(plane.shape, 1) >> 1) == p
    return jnp.where(here, pltpu.roll(plane, 2 * p + 1, 1), packed)


def pack_rows(plane, c, x, row_ref):
    last = plane.shape[0] - 1
    row_ref[0, c, pl.ds(x, 1), :] = plane[0:1]
    row_ref[1, c, pl.ds(x, 1), :] = plane[last : last + 1]


def pack_faces(planes, x, row_ref, packed):
    size_x = row_ref.shape[2]
    for c, plane in enumerate(planes):
        pack_rows(plane, c, x, row_ref)
        packed = pack_lanes(plane, c * size_x + x, packed)
    return packed


def mix_lanes(halo_ref, mix_ref):
    even = (iota(mix_ref.shape, 1) & 1) == 0
    mix_ref[...] = jnp.where(even, halo_ref[0], halo_ref[1])


def around(field_ref, row_ref, mix_ref, c, x, p):
    size_y, size_z = field_ref.shape[2:]
    row, lane = iota((size_y, size_z), 0), iota((size_y, size_z), 1)
    mid = field_ref[c, x + 1]
    low_y = jnp.where(
        row == 0,
        jnp.broadcast_to(row_ref[0, c, pl.ds(x, 1), :], mid.shape),
        pltpu.roll(mid, 1, 0),
    )
    high_y = jnp.where(
        row == size_y - 1,
        jnp.broadcast_to(row_ref[1, c, pl.ds(x, 1), :], mid.shape),
        pltpu.roll(mid, size_y - 1, 0),
    )
    ends = pltpu.roll(mix_ref[...], size_z - 1 - 2 * p, 1)
    low_z = pltpu.roll(jnp.where(lane == size_z - 1, ends, mid), 1, 1)
    high_z = pltpu.roll(jnp.where(lane == 0, ends, mid), size_z - 1, 1)
    return mid, field_ref[c, x], field_ref[c, x + 2], low_y, high_y, low_z, high_z


def lookup(tab_ref, index):
    lane, owner = index & (LANES - 1), index >> 7

    def inner(j, found):
        here = owner == j
        return tuple(
            jnp.where(
                here,
                lane_pick(jnp.broadcast_to(tab_ref[f, pl.ds(j, 1), :], index.shape), lane),
                found[f],
            )
            for f in range(5)
        )

    zero = jnp.zeros(index.shape, jnp.float32)
    return loop(tab_ref.shape[1], inner, (zero,) * 5)


def indicate(tab_ref, index, position):
    nx, ny, nz, offset, tension = lookup(tab_ref, index)
    pos_x, pos_y, pos_z = (jnp.asarray(p).astype(jnp.float32) + 0.5 for p in position)
    distance = nx * pos_x + ny * pos_y + nz * pos_z + offset
    return 0.5 * (1.0 + jnp.tanh(distance / smear_width)), tension


def nearest_plane(tab_ref, near_ref, ind_ref, ten_ref, x):
    size_y, size_z = near_ref.shape[1:]
    tall = 8 if tab_ref.shape[1] <= 8 else size_y
    for r in range(0, size_y, tall):
        here = slice(r, r + tall)
        position = (x, iota((tall, size_z), 0) + r, iota((tall, size_z), 1))
        indicator, tension = indicate(tab_ref, near_ref[x, here, :], position)
        ind_ref[0, x + 1, here, :] = indicator
        ten_ref[x, here, :] = tension


def nearest_faces(tab_ref, near_rows, near_lanes, row_ref, lane_ref):
    size_x, size_z = near_rows.shape[2:]
    size_y = near_lanes.shape[0]
    shape = (size_x, size_z)
    for side, y in ((0, 0), (1, size_y - 1)):
        position = (iota(shape, 0), y, iota(shape, 1))
        row_ref[side, 0] = indicate(tab_ref, near_rows[side, 0], position)[0]
    tall = 8 if tab_ref.shape[1] <= 8 else size_y
    for r in range(0, size_y, tall):
        here = slice(r, r + tall)
        lane = iota((tall, size_z), 1)
        position = (lane >> 1, iota((tall, size_z), 0) + r, (1 - (lane & 1)) * (size_z - 1))
        lane_ref[here, :] = indicate(tab_ref, near_lanes[here, :], position)[0]


def material(ind_ref, ten_ref, diff_ref):
    def plane(x, carry):
        indicator = ind_ref[0, x + 1]
        density = rho_liquid + (rho_gas - rho_liquid) * indicator
        viscosity = mu_liquid + (mu_gas - mu_liquid) * indicator
        share = time_step / density
        diff_ref[x] = viscosity * share
        ten_ref[x] = ten_ref[x] * (0.5 * share)
        return carry

    span(0, ten_ref.shape[0], UN_FORCE, plane, 0)


def forces(ind_ref, row_ref, mix_ref, ten_ref, force_ref, x):
    near = around(ind_ref, row_ref, mix_ref, 0, x, x)
    for a in range(3):
        force_ref[a, x] = ten_ref[x] * (near[2 * a + 2] - near[2 * a + 1])


def laplacian(old_ref, row_ref, mix_ref, c, x, p):
    mid, *near = around(old_ref, row_ref, mix_ref, c, x, p)
    return mid, near[0] + near[1] + near[2] + near[3] + near[4] + near[5] - 6.0 * mid


def advance(old_ref, row_ref, mix_ref, diff_ref, force_ref, new_ref, x):
    size_x = diff_ref.shape[0]
    diffusion = diff_ref[x]
    planes = []
    for c in range(3):
        mid, laplace = laplacian(old_ref, row_ref, mix_ref, c, x, c * size_x + x)
        planes.append(mid + (diffusion * laplace + force_ref[c, x]))
        new_ref[c, x + 1] = planes[-1]
    return planes


def advance_first(old_ref, diff_ref, force_ref, new_ref, x):
    diffusion = diff_ref[x]
    planes = []
    for c in range(3):
        planes.append(old_ref[c, x + 1] + (diffusion * new_ref[c, x + 1] + force_ref[c, x]))
        new_ref[c, x + 1] = planes[-1]
    return planes


def row_onehot(cell_ref, hot_ref):
    rows, slots = hot_ref.shape[1:]

    def each(i, carry):
        here = pl.ds(pl.multiple_of(i * LANES, LANES), LANES)
        for v in range(3):
            row = jnp.broadcast_to(cell_ref[v : v + 1, here] >> 7, (rows, LANES))
            hit = iota((rows, LANES), 0) == row
            hot_ref[v, :, here] = jnp.where(hit, 1.0, 0.0).astype(jnp.bfloat16)
        return carry

    lax.fori_loop(0, slots // LANES, each, 0)


def sample_field(vel_ref, cell_ref, hot_ref, out_ref, send, first, step):
    rows, slots = hot_ref.shape[1:]
    size_x = vel_ref.shape[1] - 2
    parts = [vel_ref[c, 1 : size_x + 1].reshape(rows, LANES).T for c in range(3)]
    field = jnp.concatenate(parts, axis=0)
    high = field.astype(jnp.bfloat16)
    low = (field - high.astype(jnp.float32)).astype(jnp.bfloat16)
    width = 256
    turns = slots // width

    def each(k, carry):
        i = (first + k * step + turns) % turns
        here = pl.ds(pl.multiple_of(i * width, width), width)
        for v in range(3):
            hot = hot_ref[v, :, here]
            got = jnp.dot(high, hot, preferred_element_type=jnp.float32)
            got = got + jnp.dot(low, hot, preferred_element_type=jnp.float32)
            lane = jnp.broadcast_to(cell_ref[v : v + 1, here] & (LANES - 1), (LANES, width))
            hit = iota((LANES, width), 0) == lane
            for c in range(3):
                picked = jnp.where(hit, got[c * LANES : (c + 1) * LANES], 0.0)
                total = jnp.sum(picked, axis=0, keepdims=True)
                for k in range(width // LANES):
                    out_ref[i * (width // LANES) + k, 3 * c + v : 3 * c + v + 1] = total[
                        :, k * LANES : (k + 1) * LANES
                    ]
        for k in range(width // LANES):
            send(i * (width // LANES) + k)
        return carry

    lax.fori_loop(0, turns, each, 0)


def invert(send_ref, inv_ref):
    tiles = inv_ref.shape[0]
    lane = iota((LANES, LANES), 1)
    place = iota((LANES, LANES), 0)
    inv_ref[...] = jnp.full(inv_ref.shape, -1, jnp.int32)

    def each(d, carry):
        listed = jnp.broadcast_to(send_ref[pl.ds(d, 1), :], (LANES, LANES)).T
        slot = place + (d * LANES + 1)

        def inner(t, carry):
            hit = jnp.where(listed - t * LANES == lane, slot, 0)
            inv_ref[pl.ds(t, 1), :] += jnp.sum(hit, axis=0, keepdims=True)
            return carry

        loop(tiles, inner, 0)
        return carry

    span(0, send_ref.shape[0], UN_INV if send_ref.shape[0] <= 8 else 1, each, 0)


def place_back(inv_ref, back_ref, out_ref):
    tall = back_ref.shape[1]

    def each(t, carry):
        index = jnp.broadcast_to(inv_ref[pl.ds(t, 1), :], (tall, LANES))
        lane, dest = index & (LANES - 1), index >> 7

        def inner(d, found):
            return jnp.where(dest == d, lane_pick(back_ref[d], lane), found)

        found = loop(back_ref.shape[0], inner, jnp.zeros((tall, LANES), jnp.float32))
        start = t * LANES if isinstance(t, int) else pl.multiple_of(t * LANES, LANES)
        out_ref[:, pl.ds(start, LANES)] = found[:9]
        return carry

    loop(inv_ref.shape[0], each, 0)


def f32(*shape):
    return jax.ShapeDtypeStruct(shape, jnp.float32)


AXES = ("gx", "gy", "gz")


def flow_kernel(
    tri_hbm,
    send_hbm,
    near_hbm,
    cell_hbm,
    vel_hbm,
    vel_out,
    ind_out,
    back_out,
    inv_out,
    tri_ref,
    send_ref,
    near_ref,
    cell_ref,
    table_ref,
    out_ref,
    arrived_ref,
    tab_ref,
    ind_ref,
    ten_ref,
    diff_ref,
    force_ref,
    state_ref,
    ind_rows,
    ind_lanes,
    ind_row_halo,
    ind_lane_halo,
    rows_ref,
    lanes_ref,
    row_halo,
    lane_halo,
    mix_ref,
    near_rows,
    near_lanes,
    hot_ref,
    inv_ref,
    sample_ref,
    back_ref,
    in_sem,
    out_sem,
    there_send,
    there_recv,
    back_send,
    back_recv,
    face_send,
    face_recv,
):
    size = {a: lax.axis_size(a) for a in AXES}
    at = {a: lax.axis_index(a) for a in AXES}
    count = size["gx"] * size["gy"]
    me = at["gx"] * size["gy"] + at["gy"]
    extent = near_ref.shape
    size_x = extent[0]

    def other(d):
        return {"gx": d // size["gy"], "gy": d % size["gy"]}

    def beside(axis, step):
        return {axis: (at[axis] + step + size[axis]) % size[axis]}

    def peers(body):
        if count <= 8:
            for r in range(1, count):
                body((me + r) % count)
        else:
            pl.loop(1, count)(lambda r: body((me + r) % count))

    loads = [
        pltpu.make_async_copy(src, dst, in_sem.at[i])
        for i, (src, dst) in enumerate(
            (
                (tri_hbm, tri_ref),
                (send_hbm, send_ref),
                (vel_hbm, state_ref.at[0, :, 1 : size_x + 1]),
                (near_hbm, near_ref),
                (cell_hbm, cell_ref),
            )
        )
    ]
    for load in loads:
        load.start()
    barrier = pltpu.get_barrier_semaphore()

    def greet(device):
        pl.semaphore_signal(
            barrier, inc=1, device_id=device, device_id_type=pl.DeviceIdType.MESH
        )

    peers(lambda d: greet(other(d)))
    greet(beside("gz", 1))
    greet(beside("gz", -1))

    def remote(src, dst, send_sem, recv_sem, device):
        return pltpu.make_async_remote_copy(
            src_ref=src,
            dst_ref=dst,
            send_sem=send_sem,
            recv_sem=recv_sem,
            device_id=device,
            device_id_type=pl.DeviceIdType.MESH,
        )

    def faces(n, field, rows, lanes, halo_rows, halo_lanes):
        pairs = (
            ("gy", 1, rows.at[1], halo_rows.at[0]),
            ("gy", -1, rows.at[0], halo_rows.at[1]),
            ("gz", 1, lanes, halo_lanes.at[0]),
            ("gz", -1, lanes, halo_lanes.at[1]),
        )
        return [
            remote(src, dst, face_send.at[n, i], face_recv.at[n, i], beside(axis, step))
            for i, (axis, step, src, dst) in enumerate(pairs, 2)
        ]

    rounds = [
        faces(
            n,
            state_ref.at[n],
            rows_ref.at[n],
            lanes_ref.at[n],
            row_halo.at[n],
            lane_halo.at[n],
        )
        for n in range(NSWEEP)
    ]
    ind_round = faces(NSWEEP, ind_ref, ind_rows, ind_lanes, ind_row_halo, ind_lane_halo)

    def x_face(n, up):
        field = ind_ref if n == NSWEEP else state_ref.at[n]
        return remote(
            field.at[:, 1 + up * (size_x - 1)],
            field.at[:, (1 - up) * (size_x + 1)],
            face_send.at[n, 1 - up],
            face_recv.at[n, 1 - up],
            beside("gx", 2 * up - 1),
        )

    def there(src, dst):
        return remote(
            out_ref.at[dst], arrived_ref.at[src], there_send.at[dst], there_recv.at[src], other(dst)
        )

    def back(src, dst):
        return remote(
            sample_ref.at[dst], back_ref.at[src], back_send.at[dst], back_recv.at[src], other(dst)
        )

    loads[0].wait()
    loads[1].wait()
    build_table(tri_ref, table_ref)
    pick_outgoing(send_ref, table_ref, out_ref)
    pl.semaphore_wait(barrier, count + 1)
    peers(lambda d: there(me, d).start())
    arrived_ref[me] = out_ref[me]

    lowest = (size["gx"] - 1 - at["gx"]) // (size["gx"] - 1)
    sides = ((1 - lowest), lowest)
    zero = jnp.zeros(extent[1:], jnp.float32)

    def first_faces(x, packed):
        planes = [state_ref[0, c, x + 1] for c in range(3)]
        return pack_faces(planes, x, rows_ref.at[0], packed)

    def near_faces(x, packed):
        return pack_faces([near_ref[x]], x, near_rows, packed)

    loads[2].wait()
    lanes_ref[0] = span(0, size_x, UN_FIRST, first_faces, zero)
    loads[4].wait()
    row_onehot(cell_ref, hot_ref)
    for up in (0, 1):
        x_face(0, up).start()
    for copy in rounds[0]:
        copy.start()
    loads[3].wait()
    near_lanes[...] = span(0, size_x, UN_FIRST, near_faces, jnp.zeros(extent[1:], jnp.int32))
    invert(send_ref, inv_ref)
    put_inv = pltpu.make_async_copy(inv_ref, inv_out, out_sem.at[3])
    put_inv.start()
    peers(lambda d: there(d, me).wait_recv())
    origin = [(at[a] * n).astype(jnp.float32) for a, n in zip(AXES, extent)]
    local_table(arrived_ref, tab_ref, origin)

    def near_plane(x, carry):
        nearest_plane(tab_ref, near_ref, ind_ref, ten_ref, x)
        return carry

    near_plane(sides[0] * (size_x - 1), 0)
    x_face(NSWEEP, sides[0]).start()
    nearest_faces(tab_ref, near_rows, near_lanes, ind_rows, ind_lanes)
    for copy in ind_round:
        copy.start()
    near_plane(sides[1] * (size_x - 1), 0)
    x_face(NSWEEP, sides[1]).start()
    span(1, size_x - 1, UN_NEAR, near_plane, 0)
    put_ind = pltpu.make_async_copy(ind_ref.at[0, 1 : size_x + 1], ind_out, out_sem.at[0])
    put_ind.start()
    material(ind_ref, ten_ref, diff_ref)
    for up in (0, 1):
        x_face(0, up).wait_recv()
    for copy in rounds[0]:
        copy.wait_recv()
    mix_lanes(lane_halo.at[0], mix_ref.at[0])

    def first_laplacian(x, carry):
        for c in range(3):
            state_ref[1, c, x + 1] = laplacian(
                state_ref.at[0], row_halo.at[0], mix_ref.at[0], c, x, c * size_x + x
            )[1]
        return carry

    span(0, size_x, UN_FIRST, first_laplacian, 0)

    for n in range(NSWEEP):
        last = n == NSWEEP - 1
        faces_in = ind_round if n == 0 else rounds[n]

        def plane(x):
            if n == 0:
                forces(ind_ref, ind_row_halo, mix_ref.at[NSWEEP], ten_ref, force_ref, x)
                return advance_first(
                    state_ref.at[0], diff_ref, force_ref, state_ref.at[1], x
                )
            return advance(
                state_ref.at[n],
                row_halo.at[n],
                mix_ref.at[n],
                diff_ref,
                force_ref,
                state_ref.at[n + 1],
                x,
            )

        def middle(x, packed):
            planes = plane(x)
            return packed if last else pack_faces(planes, x, rows_ref.at[n + 1], packed)

        for copy in faces_in:
            copy.wait_recv()
        if n == 0:
            mix_lanes(ind_lane_halo, mix_ref.at[NSWEEP])
        else:
            mix_lanes(lane_halo.at[n], mix_ref.at[n])
        packed = span(1, size_x - 1, UN_SWEEP, middle, zero)
        edges = []
        for up in reversed(sides):
            x_face(n if n else NSWEEP, 1 - up).wait_recv()
            edges.append((up * (size_x - 1), plane(up * (size_x - 1))))
            if not last:
                x_face(n + 1, up).start()
        if not last:
            for x, planes in edges:
                packed = pack_faces(planes, x, rows_ref.at[n + 1], packed)
            lanes_ref[n + 1] = packed
            for copy in rounds[n + 1]:
                copy.start()
    put_vel = pltpu.make_async_copy(
        state_ref.at[NSWEEP, :, 1 : size_x + 1], vel_out, out_sem.at[1]
    )
    put_vel.start()

    def send_back(d):
        @pl.when(d != me)
        def _():
            back(me, d).start()

    share = sample_ref.shape[0] // 2 // size["gx"]
    upper = (2 * at["gx"]) // size["gx"]
    first = (at["gx"] + upper) * share - (1 - upper)
    sample_field(
        state_ref.at[NSWEEP], cell_ref, hot_ref, sample_ref, send_back, first, 2 * upper - 1
    )
    back_ref[me] = sample_ref[me]
    peers(lambda d: back(d, me).wait_recv())
    put_back = pltpu.make_async_copy(back_ref, back_out, out_sem.at[2])
    put_back.start()
    peers(lambda d: there(me, d).wait_send())
    peers(lambda d: back(me, d).wait_send())
    for n in range(NSWEEP + 1):
        for up in (0, 1):
            x_face(n, up).wait_send()
    for group in (ind_round, *rounds):
        for copy in group:
            copy.wait_send()
    put_ind.wait()
    put_vel.wait()
    put_back.wait()
    put_inv.wait()


def finish_kernel(
    vel_hbm, ind_hbm, back_ref, inv_ref, vel_out, ind_out, vert_out, vert_ref, sem
):
    give = [
        pltpu.make_async_copy(vel_hbm, vel_out, sem.at[0]),
        pltpu.make_async_copy(ind_hbm, ind_out, sem.at[1]),
        pltpu.make_async_copy(vert_ref, vert_out, sem.at[2]),
    ]
    give[0].start()
    give[1].start()
    place_back(inv_ref, back_ref, vert_ref)
    give[2].start()
    for copy in give:
        copy.wait()


def per_device(tri_geom, send_index, near_index, return_cell, velocity):
    count = lax.axis_size("gx") * lax.axis_size("gy")
    tri_dev = tri_geom.shape[1]
    tiles = tri_dev // LANES
    size_x, size_y, size_z = near_index.shape
    slots = return_cell.shape[1]

    def vm(*shape):
        return pltpu.VMEM(shape, jnp.float32)

    dma = pltpu.SemaphoreType.DMA
    anywhere = pl.BlockSpec(memory_space=pl.ANY)
    left = pl.pallas_call(
        flow_kernel,
        out_shape=(
            f32(*velocity.shape),
            f32(*near_index.shape),
            f32(count, 16, LANES),
            jax.ShapeDtypeStruct((tiles, LANES), jnp.int32),
        ),
        in_specs=[anywhere] * 5,
        out_specs=(anywhere,) * 4,
        scratch_shapes=[
            vm(*tri_geom.shape),
            pltpu.VMEM(send_index.shape, jnp.int32),
            pltpu.VMEM(near_index.shape, jnp.int32),
            pltpu.VMEM(return_cell.shape, jnp.int32),
            vm(tiles, 8, LANES),
            vm(count, 8, LANES),
            vm(count, 8, LANES),
            vm(5, count, LANES),
            vm(1, size_x + 2, size_y, size_z),
            vm(size_x, size_y, size_z),
            vm(size_x, size_y, size_z),
            vm(3, size_x, size_y, size_z),
            vm(NSWEEP + 1, 3, size_x + 2, size_y, size_z),
            vm(2, 1, size_x, size_z),
            vm(size_y, size_z),
            vm(2, 1, size_x, size_z),
            vm(2, size_y, size_z),
            vm(NSWEEP, 2, 3, size_x, size_z),
            vm(NSWEEP, size_y, size_z),
            vm(NSWEEP, 2, 3, size_x, size_z),
            vm(NSWEEP, 2, size_y, size_z),
            vm(NSWEEP + 1, size_y, size_z),
            pltpu.VMEM((2, 1, size_x, size_z), jnp.int32),
            pltpu.VMEM((size_y, size_z), jnp.int32),
            pltpu.VMEM((3, size_x * size_y, slots), jnp.bfloat16),
            pltpu.VMEM((tiles, LANES), jnp.int32),
            vm(count, 16, LANES),
            vm(count, 16, LANES),
            dma((5,)),
            dma((4,)),
            dma((count,)),
            dma((count,)),
            dma((count,)),
            dma((count,)),
            dma((NSWEEP + 1, 6)),
            dma((NSWEEP + 1, 6)),
        ],
        compiler_params=pltpu.CompilerParams(collective_id=0, has_side_effects=True, vmem_limit_bytes=28 << 20),
        name="flow",
    )(*(pltpu.with_memory_space_constraint(x, pltpu.HBM) for x in (tri_geom, send_index, near_index, return_cell, velocity)))
    whole = pl.BlockSpec(memory_space=pltpu.VMEM)
    return pl.pallas_call(
        finish_kernel,
        out_shape=(f32(*velocity.shape), f32(*near_index.shape), f32(9, tri_dev)),
        in_specs=[anywhere, anywhere, whole, whole],
        out_specs=(anywhere,) * 3,
        scratch_shapes=[vm(9, tri_dev), dma((3,))],
        compiler_params=pltpu.CompilerParams(vmem_limit_bytes=8 << 20),
        name="finish",
    )(*left)


def solution(mesh):
    placed = (
        P(None, ("gx", "gy", "gz")),
        P(("gx", "gy", "gz"), None),
        P("gx", "gy", "gz"),
        P(None, ("gx", "gy", "gz")),
        P(None, "gx", "gy", "gz"),
    )
    return jax.shard_map(
        per_device,
        mesh=mesh,
        in_specs=placed,
        out_specs=(P(None, "gx", "gy", "gz"), P("gx", "gy", "gz"), P(None, ("gx", "gy", "gz"))),
        check_vma=False,
    )
```
